32 devices in a mesh: row: 16 (over z, y, core), col: 2 (over x).
Axes of the slice: x: 2, y: 2, z: 4, core: 2. Of those that a mesh axis runs over, the one named last changes fastest.
Arguments:
- node_features: float32 [4096, 128], P(('row', 'col')), may hold values from -6 to 6
- block_values: float32 [16, 2, 4, 128, 128], P('row', 'col')
- block_rows: int32 [16, 2, 4], P('row', 'col'), may hold values from 0 to 1, as said below
- block_cols: int32 [16, 2, 4], P('row', 'col'), may hold values from 0 to 15
- block_count: int32 [16, 2], P('row', 'col'), may hold values from 1 to 4, as said below
- w_input: float32 [128, 512], replicated, may hold values from -0.5 to 0.5
- bias_input: float32 [512], replicated, may hold values from -3 to 3
- gain_attn: float32 [512], replicated, may hold values from 0.1 to 1.9
- shift_attn: float32 [512], replicated, may hold values from -3 to 3
- w_heads: float32 [512, 1536], replicated, may hold values from -0.25 to 0.25
- w_merge: float32 [512, 512], replicated, may hold values from -0.75 to 0.75
- bias_merge: float32 [512], replicated, may hold values from -3 to 3
- gain_ffn: float32 [512], replicated, may hold values from 0.1 to 1.9
- shift_ffn: float32 [512], replicated, may hold values from -3 to 3
- w_expand: float32 [512, 1024], replicated, may hold values from -0.25 to 0.25
- bias_expand: float32 [1024], replicated, may hold values from -3 to 3
- w_reduce: float32 [1024, 512], replicated, may hold values from -0.25 to 0.25
- bias_reduce: float32 [512], replicated, may hold values from -3 to 3
- readout: float32 [512], replicated, may hold values from -0.25 to 0.25
- cotangent: float32 [4096, 512], P(('row', 'col')), may hold values from -6 to 6
Outputs:
- layer_out: float32 [4096, 512], P(('row', 'col'))
- grad_features: float32 [4096, 128], P(('row', 'col'))
- grad_w_input: float32 [128, 512], replicated
- grad_bias_input: float32 [512], replicated
- grad_gain_attn: float32 [512], replicated
- grad_shift_attn: float32 [512], replicated
- grad_w_heads: float32 [512, 1536], replicated
- grad_w_merge: float32 [512, 512], replicated
- grad_bias_merge: float32 [512], replicated
- grad_gain_ffn: float32 [512], replicated
- grad_shift_ffn: float32 [512], replicated
- grad_w_expand: float32 [512, 1024], replicated
- grad_bias_expand: float32 [1024], replicated
- grad_w_reduce: float32 [1024, 512], replicated
- grad_bias_reduce: float32 [512], replicated
- grad_readout: float32 [512], replicated
The draws below stay inside these ranges and needn't reach their ends.
Inputs may be any that keep to these rules, and one draw needn't show every extreme that they name: Within one tile the listed (block_rows, block_cols) pairs are all different. Slots 0 to block_count - 1 of a tile are live, the rest are ignored; some tile has all 4 slots live.
All inputs are finite; a program needn't handle non-finite values.
Results may differ from the reference program's by a relative error of at most 0.0003.
Values sent between devices are 32-bit elements; how exact they have to be, the bound alone decides.
No kernel may reach another device: no remote copies, remote signals or barrier semaphores. Data moves between devices by JAX's collectives and lax.ppermute only.
A program may use at most 192 MiB of HBM per device.

```python
import math
import jax
import jax.numpy as jnp
from jax import lax

D = 512
HEADS = 8
HEAD_DIM = 64
FF = 1024
HOPS = 7
F = 128
BLOCK = 128
NODE_DEV = 128
NODES = 4096
TOKENS_NODE = 8
TILE_BROWS = 2
TILE_BCOLS = 16
MAX_BLOCKS = 4
N_ROW = 16
N_COL = 2


def tile_counts(key):
    base = jax.random.fold_in(key, 11)
    tiles = N_ROW * N_COL
    levels = jax.random.randint(base, (tiles,), 20, 65)
    top_tile = jax.random.randint(jax.random.fold_in(base, 1), (), 0, tiles)
    levels = jnp.where(jnp.arange(tiles) == top_tile, 64, levels)
    counts = jnp.maximum(1, MAX_BLOCKS * levels * levels // 4096)
    return counts.reshape(N_ROW, N_COL).astype(jnp.int32)


def tile_positions(key):
    keys = jax.random.split(jax.random.fold_in(key, 23), N_ROW * N_COL)
    places = jax.vmap(lambda single: jax.random.permutation(single, TILE_BROWS * TILE_BCOLS)[:MAX_BLOCKS])(keys)
    return places.reshape(N_ROW, N_COL, MAX_BLOCKS).astype(jnp.int32)


def draw_block_count(key, part):
    return tile_counts(key)


def draw_block_rows(key, part):
    return (tile_positions(key) // TILE_BCOLS).astype(jnp.int32)


def draw_block_cols(key, part):
    return (tile_positions(key) % TILE_BCOLS).astype(jnp.int32)


def draw_block_values(key, part):
    counts = tile_counts(key).astype(jnp.float32)
    scale = jnp.sqrt(NODE_DEV / (counts * BLOCK * BLOCK))[:, :, None, None, None]
    inner = jax.random.fold_in(key, 37)
    shape = (N_ROW, N_COL, MAX_BLOCKS, BLOCK, BLOCK)
    base = jnp.clip(jax.random.normal(inner, shape, jnp.float32), -4.0, 4.0)
    return (base * scale).astype(jnp.float32)


def level_of(stream_key, shape, cuts, least, largest):
    level = 1.0
    for position, shards_of in cuts:
        draws = jax.random.uniform(jax.random.fold_in(jax.random.fold_in(stream_key, 6), position), (shards_of,), jnp.float32, least / len(cuts), largest / len(cuts))
        level = level * jnp.repeat(jnp.exp(draws), shape[position] // shards_of).reshape((-1,) + (1,) * (len(shape) - 1 - position))
    return level


def gaussian(stream_key, shape, scale, reach, pieces=(), held_as=jnp.bfloat16):
    array = jax.random.normal(stream_key, shape, jnp.float32) * scale
    if len(pieces) > 0:
        array = level_of(stream_key, shape, pieces, -0.22, 0.18) * array
    return jnp.clip(array, min=-reach, max=reach).astype(held_as)


def setup_inputs(seed: int = 0) -> dict:
    key_of = jax.random.split(jax.random.key(seed), 21)
    node_features = gaussian(key_of[0], (NODES, F), 1.0, 6.0, ((0, 32),), jnp.float32)
    block_values = draw_block_values(jax.random.fold_in(key_of[20], 71), 0)
    block_rows = draw_block_rows(jax.random.fold_in(key_of[20], 71), 0)
    block_cols = draw_block_cols(jax.random.fold_in(key_of[20], 71), 0)
    block_count = draw_block_count(jax.random.fold_in(key_of[20], 71), 0)
    w_input = gaussian(key_of[5], (F, D), F ** -0.5, 0.5, (), jnp.float32)
    bias_input = gaussian(key_of[6], (D,), 0.5, 3.0, (), jnp.float32)
    gain_attn = jnp.clip(1.0 + 0.18 * jax.random.normal(key_of[7], (D,), jnp.float32), 0.1, 1.9)
    shift_attn = gaussian(key_of[8], (D,), 0.5, 3.0, (), jnp.float32)
    w_heads = gaussian(key_of[9], (D, 3 * D), D ** -0.5, 0.25, (), jnp.float32)
    w_merge = gaussian(key_of[10], (D, D), (D // 8) ** -0.5, 0.75, (), jnp.float32)
    bias_merge = gaussian(key_of[11], (D,), 0.5, 3.0, (), jnp.float32)
    gain_ffn = jnp.clip(1.0 + 0.18 * jax.random.normal(key_of[12], (D,), jnp.float32), 0.1, 1.9)
    shift_ffn = gaussian(key_of[13], (D,), 0.5, 3.0, (), jnp.float32)
    w_expand = gaussian(key_of[14], (D, FF), D ** -0.5, 0.25, (), jnp.float32)
    bias_expand = gaussian(key_of[15], (FF,), 0.5, 3.0, (), jnp.float32)
    w_reduce = gaussian(key_of[16], (FF, D), (FF // 2) ** -0.5, 0.25, (), jnp.float32)
    bias_reduce = gaussian(key_of[17], (D,), 0.5, 3.0, (), jnp.float32)
    readout = gaussian(key_of[18], (D,), D ** -0.5, 0.25, (), jnp.float32)
    cotangent = gaussian(key_of[19], (NODES, D), 1.0, 6.0, ((0, 32),), jnp.float32)
    return dict(node_features=node_features, block_values=block_values, block_rows=block_rows, block_cols=block_cols, block_count=block_count, w_input=w_input, bias_input=bias_input, gain_attn=gain_attn, shift_attn=shift_attn, w_heads=w_heads, w_merge=w_merge, bias_merge=bias_merge, gain_ffn=gain_ffn, shift_ffn=shift_ffn, w_expand=w_expand, bias_expand=bias_expand, w_reduce=w_reduce, bias_reduce=bias_reduce, readout=readout, cotangent=cotangent)


@jax.custom_vjp
def low(v):
    return lax.optimization_barrier(v.astype(jnp.bfloat16)).astype(jnp.float32)

@jax.custom_vjp
def low_back(v):
    return v

def low_keep(v):
    return (low(v), None)

def low_pass(kept, grad):
    return (grad,)

def back_keep(v):
    return (v, None)

def back_low(kept, grad):
    return (low(grad),)
low.defvjp(low_keep, low_pass)
low_back.defvjp(back_keep, back_low)
exact = lax.Precision.HIGHEST

def layer_norm(values, gain, shift):
    average = lax.optimization_barrier(jnp.mean(values, axis=-1, keepdims=True))
    centred = values - average
    spread = lax.optimization_barrier(jnp.mean(centred * centred, axis=-1, keepdims=True))
    return centred * lax.rsqrt(spread + 1e-05) * gain + shift

def node_tail(start, gain_attn, shift_attn, w_heads, w_merge, bias_merge, gain_ffn, shift_ffn, w_expand, bias_expand, w_reduce, bias_reduce, readout):
    node_count, token_count, columns = start.shape
    normed = layer_norm(start, gain_attn, shift_attn)
    projected = jnp.einsum('ntd,de->nte', normed, w_heads, precision=exact)
    queries = projected[..., :columns].reshape(node_count, token_count, HEADS, HEAD_DIM)
    key_rows = projected[..., columns:2 * columns].reshape(node_count, token_count, HEADS, HEAD_DIM)
    value_rows = projected[..., 2 * columns:].reshape(node_count, token_count, HEADS, HEAD_DIM)
    scores = jnp.einsum('nqhe,nkhe->nhqk', queries, key_rows, precision=exact) / math.sqrt(HEAD_DIM)
    attention = jax.nn.softmax(scores, axis=-1)
    mixed = jnp.einsum('nhqk,nkhe->nqhe', attention, value_rows, precision=exact).reshape(node_count, token_count, columns)
    middle = start + jnp.einsum('ntd,de->nte', mixed, w_merge, precision=exact) + bias_merge
    normed_two = layer_norm(middle, gain_ffn, shift_ffn)
    activated = jax.nn.gelu(jnp.einsum('ntd,de->nte', normed_two, w_expand, precision=exact) + bias_expand, approximate=False)
    final = middle + jnp.einsum('nte,ed->ntd', activated, w_reduce, precision=exact) + bias_reduce
    center = final[:, 0]
    others = final[:, 1:]
    weights = jax.nn.softmax(jnp.einsum('nkd,d->nk', others, readout, precision=exact), axis=-1)
    return center + jnp.einsum('nk,nkd->nd', weights, others, precision=exact)

def propagate(field, block_values, block_rows, block_cols, block_count):
    columns = field.shape[1]
    column_parts = field.reshape(N_ROW, N_COL, NODE_DEV, columns).transpose(1, 0, 2, 3).reshape(N_COL, TILE_BCOLS, BLOCK, columns)
    tile_index = jnp.arange(N_COL).astype(jnp.int32)[:, None]

    def tile_row(row_index):
        values = block_values[row_index]
        row_ids = block_rows[row_index]
        col_ids = block_cols[row_index]
        counts = block_count[row_index]
        is_live = (jnp.arange(MAX_BLOCKS).astype(jnp.int32)[None, :] < counts[:, None]).astype(field.dtype)
        picked = column_parts[tile_index, col_ids]
        products = jnp.einsum('cbij,cbjw->cbiw', values, picked, precision=exact)
        row_table = (row_ids[:, :, None] == jnp.arange(TILE_BROWS).astype(jnp.int32)[None, None, :]).astype(field.dtype) * is_live[:, :, None]
        summed = jnp.einsum('cbr,cbiw->riw', row_table, products, precision=exact)
        return summed.reshape(TILE_BROWS * BLOCK, columns)
    rows_out = lax.map(jax.checkpoint(tile_row), jnp.arange(N_ROW).astype(jnp.int32))
    return rows_out.reshape(NODES, columns)

def reference(node_features, block_values, block_rows, block_cols, block_count, w_input, bias_input, gain_attn, shift_attn, w_heads, w_merge, bias_merge, gain_ffn, shift_ffn, w_expand, bias_expand, w_reduce, bias_reduce, readout, cotangent):
    group = math.gcd(NODES, 512)

    def forward(features, w_input, bias_input, gain_attn, shift_attn, w_heads, w_merge, bias_merge, gain_ffn, shift_ffn, w_expand, bias_expand, w_reduce, bias_reduce, readout):
        hop_list = [features]
        for hop_index in range(HOPS):
            hop_list.append(propagate(hop_list[-1], block_values, block_rows, block_cols, block_count))
        stacked = jnp.stack(hop_list, axis=1).reshape(NODES // group, group, TOKENS_NODE, F)

        def node_group(span_rows):
            start = jnp.einsum('ntf,fd->ntd', span_rows, w_input, precision=exact) + bias_input
            return node_tail(start, gain_attn, shift_attn, w_heads, w_merge, bias_merge, gain_ffn, shift_ffn, w_expand, bias_expand, w_reduce, bias_reduce, readout)
        result = lax.map(jax.checkpoint(node_group), stacked)
        return result.reshape(NODES, D)
    layer_out, pullback = jax.vjp(forward, node_features, w_input, bias_input, gain_attn, shift_attn, w_heads, w_merge, bias_merge, gain_ffn, shift_ffn, w_expand, bias_expand, w_reduce, bias_reduce, readout)
    gradients = pullback(cotangent)
    return (layer_out, gradients[0], gradients[1], gradients[2], gradients[3], gradients[4], gradients[5], gradients[6], gradients[7], gradients[8], gradients[9], gradients[10], gradients[11], gradients[12], gradients[13], gradients[14])
```

```python
import functools
import math

import jax
import jax.numpy as jnp
from jax import lax
from jax.experimental import pallas as pl
from jax.experimental.pallas import tpu as pltpu
from jax.sharding import PartitionSpec as P

HEADS = 8
HEAD_DIM = 64
HOPS = 7


exact = lax.Precision.HIGHEST
near = lax.Precision.HIGH
AXES = ("row", "col")
LANES = 128
PIECE = 4
UNROLL = 4


def block_list(meta_ref, source, taken, given, slots, n_col, row_blocks):
    def tile(position, live):
        row, col = position // n_col, position % n_col
        count = meta_ref[position, 2 * slots]
        for slot in range(slots):
            source[live] = position * slots + slot
            given[live] = row * row_blocks + meta_ref[position, slot]
            taken[live] = meta_ref[position, slots + slot] * n_col + col
            live = live + jnp.where(slot < count, 1, 0)
        return live

    tiles = meta_ref.shape[0]
    live = lax.fori_loop(0, tiles, tile, jnp.int32(0))
    for extra in range(UNROLL):
        source[live + extra] = 0
        given[live + extra] = tiles
        taken[live + extra] = tiles
    return (live + UNROLL - 1) // UNROLL


def walk_kernel(
    forward, hops, slots, n_col, row_blocks, meta_ref, field_ref, values_ref, out_ref, upper, lower, total, state, source, taken, given
):
    if forward:
        steps = block_list(meta_ref, source, taken, given, slots, n_col, row_blocks)
    else:
        steps = block_list(meta_ref, source, given, taken, slots, n_col, row_blocks)
    blocks = field_ref.shape[0]

    def split(step, _):
        for inner in range(UNROLL):
            place = step * UNROLL + inner
            block = values_ref[source[place]]
            rounded = block.astype(jnp.bfloat16)
            upper[place] = rounded
            lower[place] = (block - rounded.astype(jnp.float32)).astype(jnp.bfloat16)
        return 0

    lax.fori_loop(0, steps, split, 0)
    state[blocks] = jnp.zeros_like(state[blocks])
    is_top = lax.broadcasted_iota(jnp.int32, (blocks, 2 * PIECE, LANES), 1) < PIECE

    def keep(field):
        doubled = jnp.concatenate([field, field], axis=1)
        rounded = doubled.astype(jnp.bfloat16).astype(jnp.float32)
        state[:blocks] = jnp.where(is_top, rounded, doubled - rounded)

    def apply():
        total[...] = jnp.zeros_like(total)

        def some(step, _):
            products = []
            for inner in range(UNROLL):
                place = step * UNROLL + inner
                rows = state[taken[place]].astype(jnp.bfloat16)
                axis = 1 if forward else 0
                dims = (((1,), (axis,)), ((), ()))
                products.append(
                    lax.dot_general(rows, upper[place], dims, preferred_element_type=jnp.float32)
                    + lax.dot_general(rows, lower[place], dims, preferred_element_type=jnp.float32)
                )
            for inner in range(UNROLL):
                target = given[step * UNROLL + inner]
                total[target] = total[target] + products[inner]
            return 0

        lax.fori_loop(0, steps, some, 0)
        summed = total[:blocks]
        return summed[:, :PIECE] + summed[:, PIECE:]

    if forward:
        field = field_ref[:, :PIECE]
        out_ref[:, :PIECE] = field
        keep(field)
        for hop in range(1, hops + 1):
            field = apply()
            out_ref[:, hop * PIECE : (hop + 1) * PIECE] = field
            if hop < hops:
                keep(field)
    else:
        field = field_ref[:, hops * PIECE :]
        for hop in range(hops - 1, -1, -1):
            keep(field)
            field = apply()
            if hop > 0:
                field = field + field_ref[:, hop * PIECE : (hop + 1) * PIECE]
        out_ref[:, :PIECE] = field
        out_ref[:, PIECE:] = field


def walk(forward, meta, field, values, n_col, row_blocks):
    blocks = field.shape[0]
    slots = values.shape[0] // meta.shape[0]
    room = values.shape[0] + UNROLL
    out_rows = (HOPS + 1) * PIECE if forward else 2 * PIECE
    return pl.pallas_call(
        functools.partial(walk_kernel, forward, HOPS, slots, n_col, row_blocks),
        out_shape=jax.ShapeDtypeStruct((blocks, out_rows, LANES), jnp.float32),
        in_specs=[
            pl.BlockSpec(memory_space=pltpu.SMEM),
            pl.BlockSpec(memory_space=pltpu.VMEM),
            pl.BlockSpec(memory_space=pltpu.VMEM),
        ],
        out_specs=pl.BlockSpec(memory_space=pltpu.VMEM),
        scratch_shapes=[
            pltpu.VMEM((room, LANES, LANES), jnp.bfloat16),
            pltpu.VMEM((room, LANES, LANES), jnp.bfloat16),
            pltpu.VMEM((blocks + 1, 2 * PIECE, LANES), jnp.float32),
            pltpu.VMEM((blocks + 1, 2 * PIECE, LANES), jnp.float32),
            pltpu.SMEM((room,), jnp.int32),
            pltpu.SMEM((room,), jnp.int32),
            pltpu.SMEM((room,), jnp.int32),
        ],
        compiler_params=pltpu.CompilerParams(vmem_limit_bytes=48 << 20),
        name="walk_forward" if forward else "walk_backward",
    )(meta, field, values)


def layer_norm(values, gain, shift):
    average = jnp.mean(values, axis=-1, keepdims=True)
    centred = values - average
    spread = jnp.mean(centred * centred, axis=-1, keepdims=True)
    return centred * lax.rsqrt(spread + 1e-05) * gain + shift


def node_tail(
    start,
    gain_attn,
    shift_attn,
    w_heads,
    w_merge,
    bias_merge,
    gain_ffn,
    shift_ffn,
    w_expand,
    bias_expand,
    w_reduce,
    bias_reduce,
    readout,
):
    node_count, token_count, columns = start.shape
    normed = layer_norm(start, gain_attn, shift_attn)
    projected = jnp.einsum("ntd,de->nte", normed, w_heads, precision=near)
    queries = projected[..., :columns].reshape(node_count, token_count, HEADS, HEAD_DIM)
    key_rows = projected[..., columns : 2 * columns].reshape(
        node_count, token_count, HEADS, HEAD_DIM
    )
    value_rows = projected[..., 2 * columns :].reshape(node_count, token_count, HEADS, HEAD_DIM)
    scores = jnp.einsum("nqhe,nkhe->nhqk", queries, key_rows, precision=near) / math.sqrt(HEAD_DIM)
    attention = jax.nn.softmax(scores, axis=-1)
    mixed = jnp.einsum("nhqk,nkhe->nqhe", attention, value_rows, precision=near).reshape(
        node_count, token_count, columns
    )
    middle = start + jnp.einsum("ntd,de->nte", mixed, w_merge, precision=near) + bias_merge
    normed_two = layer_norm(middle, gain_ffn, shift_ffn)
    activated = jax.nn.gelu(
        jnp.einsum("ntd,de->nte", normed_two, w_expand, precision=near) + bias_expand,
        approximate=False,
    )
    final = middle + jnp.einsum("nte,ed->ntd", activated, w_reduce, precision=near) + bias_reduce
    center = final[:, 0]
    others = final[:, 1:]
    weights = jax.nn.softmax(jnp.einsum("nkd,d->nk", others, readout, precision=near), axis=-1)
    return center + jnp.einsum("nk,nkd->nd", weights, others, precision=near)


def per_device(
    node_features,
    block_values,
    block_rows,
    block_cols,
    block_count,
    w_input,
    bias_input,
    gain_attn,
    shift_attn,
    w_heads,
    w_merge,
    bias_merge,
    gain_ffn,
    shift_ffn,
    w_expand,
    bias_expand,
    w_reduce,
    bias_reduce,
    readout,
    cotangent,
):
    values = block_values[0, 0]
    row_ids = block_rows[0, 0]
    col_ids = block_cols[0, 0]
    block_size = values.shape[-1]
    node_count = node_features.shape[0]
    row_blocks = lax.axis_size("col") * node_count // block_size
    col_blocks = lax.axis_size("row") * node_count // block_size
    is_live = (jnp.arange(values.shape[0]) < block_count[0, 0]).astype(jnp.float32)
    row_table = (row_ids[:, None] == jnp.arange(row_blocks)[None, :]).astype(jnp.float32) * is_live[
        :, None
    ]
    col_table = (col_ids[:, None] == jnp.arange(col_blocks)[None, :]).astype(jnp.float32) * is_live[
        :, None
    ]
    devices = lax.axis_size("row") * lax.axis_size("col")
    whole = (
        block_size == LANES
        and node_count == LANES
        and node_features.shape[1] == PIECE * devices
        and devices * values.size * 4 <= 16 << 20
    )
    if whole:
        n_col = lax.axis_size("col")
        everything = lax.all_gather(values, AXES, axis=0, tiled=True)
        places = jnp.concatenate([row_ids, col_ids, block_count[0]]).astype(jnp.float32)
        note = jnp.zeros((PIECE, LANES), jnp.float32).at[0, : places.shape[0]].set(places)
        sent = jnp.concatenate(
            [
                node_features.T.reshape(devices, PIECE, LANES),
                jnp.broadcast_to(note[None], (devices, PIECE, LANES)),
            ],
            axis=1,
        )
        taken = lax.all_to_all(sent, AXES, 0, 0, tiled=True)
        meta = taken[:, PIECE, : places.shape[0]].astype(jnp.int32)
        walked = walk(True, meta, taken, everything, n_col, row_blocks)
        walked = lax.all_to_all(walked, AXES, 0, 0, tiled=True)
        stacked = walked.reshape(devices, HOPS + 1, PIECE, LANES).transpose(3, 1, 0, 2)
        stacked = stacked.reshape(LANES, HOPS + 1, devices * PIECE)
    else:
        hop_list = [node_features]
        for hop_index in range(HOPS):
            field = hop_list[-1]
            forward_columns = field.shape[1]
            forward_gathered = lax.all_gather(field, "row", axis=0, tiled=True).reshape(
                col_blocks, block_size, forward_columns
            )
            forward_picked = forward_gathered[col_ids]
            forward_products = jnp.einsum("bij,bjw->biw", values, forward_picked, precision=exact)
            forward_partial_value = jnp.einsum(
                "br,biw->riw", row_table, forward_products, precision=exact
            ).reshape(row_blocks * block_size, forward_columns)
            hop_list.append(
                lax.psum_scatter(forward_partial_value, "col", scatter_dimension=0, tiled=True)
            )
        stacked = jnp.stack(hop_list, axis=1)

    def local_layer(
        stacked_hops,
        w_input,
        bias_input,
        gain_attn,
        shift_attn,
        w_heads,
        w_merge,
        bias_merge,
        gain_ffn,
        shift_ffn,
        w_expand,
        bias_expand,
        w_reduce,
        bias_reduce,
        readout,
    ):
        start = jnp.einsum("ntf,fd->ntd", stacked_hops, w_input, precision=near) + bias_input
        return node_tail(
            start,
            gain_attn,
            shift_attn,
            w_heads,
            w_merge,
            bias_merge,
            gain_ffn,
            shift_ffn,
            w_expand,
            bias_expand,
            w_reduce,
            bias_reduce,
            readout,
        )

    layer_out, pullback = jax.vjp(
        local_layer,
        stacked,
        w_input,
        bias_input,
        gain_attn,
        shift_attn,
        w_heads,
        w_merge,
        bias_merge,
        gain_ffn,
        shift_ffn,
        w_expand,
        bias_expand,
        w_reduce,
        bias_reduce,
        readout,
    )
    (
        grad_hops,
        grad_w_input,
        grad_bias_input,
        grad_gain_attn,
        grad_shift_attn,
        grad_w_heads,
        grad_w_merge,
        grad_bias_merge,
        grad_gain_ffn,
        grad_shift_ffn,
        grad_w_expand,
        grad_bias_expand,
        grad_w_reduce,
        grad_bias_reduce,
        grad_readout,
    ) = pullback(cotangent)
    if whole:
        sent = grad_hops.reshape(LANES, HOPS + 1, devices, PIECE).transpose(2, 1, 3, 0)
        sent = sent.reshape(devices, (HOPS + 1) * PIECE, LANES)
        back = lax.all_to_all(sent, AXES, 0, 0, tiled=True)
        back = walk(False, meta, back, everything, n_col, row_blocks)
        back = lax.all_to_all(back, AXES, 0, 0, tiled=True)[:, :PIECE]
        carried = grad_hops[:, 0] + back.reshape(devices * PIECE, LANES).T
    else:
        carried = grad_hops[:, HOPS]
        for hop_index in range(HOPS - 1, -1, -1):
            columns = carried.shape[1]
            gathered = lax.all_gather(carried, "col", axis=0, tiled=True).reshape(
                row_blocks, block_size, columns
            )
            picked = gathered[row_ids]
            products = jnp.einsum("bji,bjw->biw", values, picked, precision=exact)
            partial_value = jnp.einsum("bc,biw->ciw", col_table, products, precision=exact).reshape(
                col_blocks * block_size, columns
            )
            carried = grad_hops[:, hop_index] + lax.psum_scatter(
                partial_value, "row", scatter_dimension=0, tiled=True
            )
    summed = lax.psum(
        (
            grad_w_input,
            grad_bias_input,
            grad_gain_attn,
            grad_shift_attn,
            grad_w_heads,
            grad_w_merge,
            grad_bias_merge,
            grad_gain_ffn,
            grad_shift_ffn,
            grad_w_expand,
            grad_bias_expand,
            grad_w_reduce,
            grad_bias_reduce,
            grad_readout,
        ),
        ("row", "col"),
    )
    return (
        layer_out,
        carried,
        summed[0],
        summed[1],
        summed[2],
        summed[3],
        summed[4],
        summed[5],
        summed[6],
        summed[7],
        summed[8],
        summed[9],
        summed[10],
        summed[11],
        summed[12],
        summed[13],
    )


def solution(mesh):
    placed = (
        P(("row", "col"), None),
        P("row", "col", None, None, None),
        P("row", "col", None),
        P("row", "col", None),
        P("row", "col"),
        P(),
        P(),
        P(),
        P(),
        P(),
        P(),
        P(),
        P(),
        P(),
        P(),
        P(),
        P(),
        P(),
        P(),
        P(("row", "col"), None),
    )
    return jax.shard_map(
        per_device,
        mesh=mesh,
        in_specs=placed,
        out_specs=(
            P(("row", "col"), None),
            P(("row", "col"), None),
            P(),
            P(),
            P(),
            P(),
            P(),
            P(),
            P(),
            P(),
            P(),
            P(),
            P(),
            P(),
            P(),
            P(),
        ),
        check_vma=False,
    )
```

```python
import functools
import math

import jax
import jax.numpy as jnp
from jax import lax
from jax.experimental import pallas as pl
from jax.experimental.pallas import tpu as pltpu
from jax.sharding import PartitionSpec as P

HEADS = 8
HEAD_DIM = 64
HOPS = 7
TOKENS = HOPS + 1


exact = lax.Precision.HIGHEST
AXES = ("row", "col")
LANES = 128
PIECE = 4
UNROLL = 16
NODES_STEP = 32


def block_list(meta_ref, source, taken, given, slots, n_col, row_blocks):
    def tile(position, live):
        row, col = position // n_col, position % n_col
        count = meta_ref[position, 2 * slots]
        for slot in range(slots):
            source[live] = position * slots + slot
            given[live] = row * row_blocks + meta_ref[position, slot]
            taken[live] = meta_ref[position, slots + slot] * n_col + col
            live = live + jnp.where(slot < count, 1, 0)
        return live

    tiles = meta_ref.shape[0]
    live = lax.fori_loop(0, tiles, tile, jnp.int32(0))
    for extra in range(UNROLL):
        source[live + extra] = 0
        given[live + extra] = tiles
        taken[live + extra] = tiles
    return (live + UNROLL - 1) // UNROLL


def walk_kernel(
    forward, hops, slots, n_col, row_blocks, meta_ref, field_ref, values_ref, out_ref, pairs, total, state, source, taken, given
):
    if forward:
        steps = block_list(meta_ref, source, taken, given, slots, n_col, row_blocks)
    else:
        steps = block_list(meta_ref, source, given, taken, slots, n_col, row_blocks)
    blocks = field_ref.shape[0]

    def split_some(step, _):
        for inner in range(4):
            place = step * 4 + inner
            block = values_ref[source[place]]
            upper, lower = split(block.T if forward else block)
            pairs[place, :LANES] = upper
            pairs[place, LANES:] = lower
        return 0

    lax.fori_loop(0, steps * (UNROLL // 4), split_some, 0)
    state[blocks] = jnp.zeros_like(state[blocks])
    is_top = lax.broadcasted_iota(jnp.int32, (blocks, 2 * PIECE, LANES), 1) < PIECE

    def keep(field):
        doubled = jnp.concatenate([field, field], axis=1)
        rounded = doubled.astype(jnp.bfloat16).astype(jnp.float32)
        state[:blocks] = jnp.where(is_top, rounded, doubled - rounded)

    def apply():
        total[...] = jnp.zeros_like(total)

        def some(step, _):
            products = []
            for inner in range(UNROLL):
                place = step * UNROLL + inner
                rows = state[taken[place]].astype(jnp.bfloat16)
                rows = jnp.concatenate([rows, rows], axis=1)
                products.append(dot(rows, pairs[place], 1, 0))
            for inner in range(UNROLL):
                target = given[step * UNROLL + inner]
                total[target] = total[target] + products[inner]
            return 0

        lax.fori_loop(0, steps, some, 0)
        summed = total[:blocks]
        return summed[:, :PIECE] + summed[:, PIECE:]

    if forward:
        field = field_ref[:, :PIECE]
        out_ref[:, :PIECE] = field
        keep(field)
        for hop in range(1, hops + 1):
            field = apply()
            out_ref[:, hop * PIECE : (hop + 1) * PIECE] = field
            if hop < hops:
                keep(field)
    else:
        field = field_ref[:, hops * PIECE :]
        for hop in range(hops - 1, -1, -1):
            keep(field)
            field = apply()
            if hop > 0:
                field = field + field_ref[:, hop * PIECE : (hop + 1) * PIECE]
        out_ref[:, :PIECE] = field
        out_ref[:, PIECE:] = field


def walk(forward, meta, field, values, n_col, row_blocks):
    blocks = field.shape[0]
    slots = values.shape[0] // meta.shape[0]
    room = values.shape[0] + UNROLL
    out_rows = (HOPS + 1) * PIECE if forward else 2 * PIECE
    return pl.pallas_call(
        functools.partial(walk_kernel, forward, HOPS, slots, n_col, row_blocks),
        out_shape=jax.ShapeDtypeStruct((blocks, out_rows, LANES), jnp.float32),
        in_specs=[
            pl.BlockSpec(memory_space=pltpu.SMEM),
            pl.BlockSpec(memory_space=pltpu.VMEM),
            pl.BlockSpec(memory_space=pltpu.VMEM),
        ],
        out_specs=pl.BlockSpec(memory_space=pltpu.VMEM),
        scratch_shapes=[
            pltpu.VMEM((room, 2 * LANES, LANES), jnp.bfloat16),
            pltpu.VMEM((blocks + 1, 2 * PIECE, LANES), jnp.float32),
            pltpu.VMEM((blocks + 1, 2 * PIECE, LANES), jnp.float32),
            pltpu.SMEM((room,), jnp.int32),
            pltpu.SMEM((room,), jnp.int32),
            pltpu.SMEM((room,), jnp.int32),
        ],
        compiler_params=pltpu.CompilerParams(vmem_limit_bytes=48 << 20),
        cost_estimate=work(20),
        name="walk_forward" if forward else "walk_backward",
    )(meta, field, values)


def work(microseconds):
    return pl.CostEstimate(
        flops=microseconds * 1_000_000_000,
        bytes_accessed=microseconds * 3_000_000,
        transcendentals=0,
    )


def split(values):
    upper = values.astype(jnp.bfloat16)
    return upper, (values - upper.astype(jnp.float32)).astype(jnp.bfloat16)


def dot(left, right, left_axis, right_axis):
    return lax.dot_general(
        left, right, (((left_axis,), (right_axis,)), ((), ())), preferred_element_type=jnp.float32
    )


def product(left, right, left_axis, right_axis):
    return dot(
        jnp.concatenate([left[0], left[0], left[1]], axis=left_axis),
        jnp.concatenate([right[0], right[1], right[0]], axis=right_axis),
        left_axis,
        right_axis,
    )


def pair(upper_ref, lower_ref):
    return upper_ref[...], lower_ref[...]


def standard(values):
    centred = values - jnp.mean(values, axis=-1, keepdims=True)
    scale = lax.rsqrt(jnp.mean(centred * centred, axis=-1, keepdims=True) + 1e-05)
    return centred * scale, scale


def standard_back(upstream, normed, scale):
    average = jnp.mean(upstream, axis=-1, keepdims=True)
    along = jnp.mean(upstream * normed, axis=-1, keepdims=True)
    return (upstream - average - normed * along) * scale


def column_sum(values):
    return jnp.sum(values, axis=0, keepdims=True)


def head_tables(columns):
    row = lax.broadcasted_iota(jnp.int32, (columns, LANES), 0) // HEAD_DIM
    lane = lax.broadcasted_iota(jnp.int32, (columns, LANES), 1) % HEADS
    gather = jnp.where(row == lane, 1.0, 0.0).astype(jnp.bfloat16)
    row = lax.broadcasted_iota(jnp.int32, (LANES, columns), 0) % HEADS
    lane = lax.broadcasted_iota(jnp.int32, (LANES, columns), 1) // HEAD_DIM
    spread = jnp.where(row == lane, 1.0, 0.0).astype(jnp.bfloat16)
    return gather, spread


def per_head(values, gather):
    upper, lower = split(values)
    return dot(
        jnp.concatenate([upper, lower], axis=1), jnp.concatenate([gather, gather], axis=0), 1, 0
    )


def over_columns(values, spread):
    upper, lower = split(values)
    return dot(
        jnp.concatenate([upper, lower], axis=1), jnp.concatenate([spread, spread], axis=0), 1, 0
    )


def lane_group(rows):
    return lax.broadcasted_iota(jnp.int32, (rows, LANES), 1) // HEADS


def token_scores(left, right, gather, nodes, columns):
    group = lane_group(nodes)
    kept = [jnp.zeros((nodes, LANES), jnp.float32) for _ in range(TOKENS // 2)]
    for key in range(TOKENS):
        sums = per_head((left() * right(key)[None]).reshape(TOKENS * nodes, columns), gather)
        for query in range(TOKENS):
            part = sums[query * nodes : (query + 1) * nodes]
            kept[query // 2] = jnp.where(group == 2 * key + query % 2, part, kept[query // 2])
    return jnp.concatenate(kept, axis=0)


def over_keys(values, combine):
    for shift in (2 * HEADS, 4 * HEADS, 8 * HEADS):
        values = combine(values, pltpu.roll(values, shift, 1))
    return values


def one_key(table, key, spread, nodes):
    group = lane_group(nodes)
    rows = [
        jnp.where(
            group == 2 * key + query % 2,
            table[(query // 2) * nodes : (query // 2 + 1) * nodes],
            0.0,
        )
        for query in range(TOKENS)
    ]
    return over_columns(jnp.concatenate(rows, axis=0), spread)


def front_kernel(
    hops_ref,
    cotangent_ref,
    wi_h,
    wi_l,
    wh_h,
    wh_l,
    wm_h,
    wm_l,
    we_h,
    we_l,
    wr_h,
    wr_l,
    bias_input,
    gain_attn,
    shift_attn,
    bias_merge,
    gain_ffn,
    shift_ffn,
    bias_expand,
    bias_reduce,
    readout,
    out_ref,
    z0_ref,
    heads_ref,
    probs_ref,
    mixed_ref,
    dz1_ref,
    first,
    second,
    small,
    u_h,
    u_l,
    a_h,
    a_l,
    d_h,
    d_l,
    slope,
    z1_ref,
    n2_ref,
):
    nodes = hops_ref.shape[1]
    rows = TOKENS * nodes
    columns = z0_ref.shape[2]

    @pl.when(pl.program_id(0) == 0)
    def _():
        first[...] = jnp.zeros_like(first)
        second[...] = jnp.zeros_like(second)
        small[...] = jnp.zeros_like(small)

    def by_token(values):
        return values.reshape(TOKENS, nodes, values.shape[-1])

    hops = split(hops_ref[...].reshape(rows, hops_ref.shape[2]))
    z0 = product(hops, pair(wi_h, wi_l), 1, 0) + bias_input[...]
    z0_ref[...] = by_token(z0)
    n1, _ = standard(z0)
    u_h[...], u_l[...] = split(n1 * gain_attn[...] + shift_attn[...])
    heads_ref[...] = by_token(product(pair(u_h, u_l), pair(wh_h, wh_l), 1, 0))
    gather, spread = head_tables(columns)
    scores = token_scores(
        lambda: heads_ref[:, :, :columns],
        lambda key: heads_ref[key, :, columns : 2 * columns],
        gather,
        nodes,
        columns,
    ) * (1.0 / math.sqrt(HEAD_DIM))
    raised = jnp.exp(scores - over_keys(scores, jnp.maximum))
    probs = raised / over_keys(raised, jnp.add)
    probs_ref[...] = probs.reshape(TOKENS // 2, nodes, LANES)
    for key in range(TOKENS):
        term = by_token(one_key(probs, key, spread, nodes)) * heads_ref[key, :, 2 * columns :][None]
        mixed_ref[...] = term if key == 0 else mixed_ref[...] + term
    u_h[...], u_l[...] = split(mixed_ref[...].reshape(rows, columns))
    z1 = (
        z0_ref[...].reshape(rows, columns)
        + product(pair(u_h, u_l), pair(wm_h, wm_l), 1, 0)
        + bias_merge[...]
    )
    z1_ref[...] = z1
    n2, scale = standard(z1)
    n2_ref[...] = n2
    u_h[...], u_l[...] = split(n2 * gain_ffn[...] + shift_ffn[...])
    pre = product(pair(u_h, u_l), pair(we_h, we_l), 1, 0) + bias_expand[...]
    below = 0.5 * (1.0 + lax.erf(pre * math.sqrt(0.5)))
    slope[...] = below + pre * jnp.exp(-0.5 * pre * pre) * (1.0 / math.sqrt(2.0 * math.pi))
    a_h[...], a_l[...] = split(pre * below)
    z2 = by_token(
        z1_ref[...] + product(pair(a_h, a_l), pair(wr_h, wr_l), 1, 0) + bias_reduce[...]
    )
    marks = jnp.sum(z2[1:] * readout[...][None], axis=-1, keepdims=True)
    raised = jnp.exp(marks - jnp.max(marks, axis=0, keepdims=True))
    alpha = raised / jnp.sum(raised, axis=0, keepdims=True)
    out_ref[...] = z2[0] + jnp.sum(alpha * z2[1:], axis=0)
    cotangent = cotangent_ref[...]
    along = jnp.sum(cotangent[None] * z2[1:], axis=-1, keepdims=True)
    slant = alpha * (along - jnp.sum(alpha * along, axis=0, keepdims=True))
    small[0:1] += column_sum(jnp.sum(slant * z2[1:], axis=0))
    dz2 = jnp.concatenate(
        [cotangent[None], alpha * cotangent[None] + slant * readout[...][None]], axis=0
    ).reshape(rows, columns)
    dz1_ref[...] = by_token(dz2)
    d_h[:, :columns], d_l[:, :columns] = split(dz2)
    small[1:2] += column_sum(dz2)
    near = (d_h[:, :columns], d_l[:, :columns])
    wide = a_h.shape[1]
    first[:wide] += product(pair(a_h, a_l), near, 0, 0)
    dpre = product(near, pair(wr_h, wr_l), 1, 1) * slope[...]
    total = column_sum(dpre)
    small[2:3] += total[:, :columns]
    small[5:6] += total[:, columns:]
    d_h[...], d_l[...] = split(dpre)
    grown = product(pair(u_h, u_l), pair(d_h, d_l), 0, 0)
    second[:columns] += grown[:, :columns]
    second[columns : 2 * columns] += grown[:, columns:]
    du2 = product(pair(d_h, d_l), pair(we_h, we_l), 1, 1)
    n2 = n2_ref[...]
    small[3:4] += column_sum(du2 * n2)
    small[4:5] += column_sum(du2)
    dz1 = dz1_ref[...].reshape(rows, columns) + standard_back(du2 * gain_ffn[...], n2, scale)
    dz1_ref[...] = by_token(dz1)
    d_h[:, :columns], d_l[:, :columns] = split(dz1)
    u_h[...], u_l[...] = split(mixed_ref[...].reshape(rows, columns))
    grown = product(pair(u_h, u_l), (d_h[:, :columns], d_l[:, :columns]), 0, 0)
    first[wide:] += grown[: columns // 2]
    second[2 * columns :] += grown[columns // 2 :]
    small[6:7] += column_sum(dz1)


def attention_back_kernel(*refs):
    heads_ref, probs_ref, dz1_ref, wm_h, wm_l = refs[:5]
    back_h, back_l, dmixed_ref, dheads_ref = refs[-4:]
    nodes = dz1_ref.shape[1]
    rows = TOKENS * nodes
    columns = dz1_ref.shape[2]

    def by_token(values):
        return values.reshape(TOKENS, nodes, values.shape[-1])

    dz1 = split(dz1_ref[...].reshape(rows, columns))
    dmixed_ref[...] = by_token(product(dz1, pair(wm_h, wm_l), 1, 1))
    gather, spread = head_tables(columns)
    probs = probs_ref[...].reshape(TOKENS // 2 * nodes, LANES)
    dprobs = token_scores(
        lambda: dmixed_ref[...],
        lambda key: heads_ref[key, :, 2 * columns :],
        gather,
        nodes,
        columns,
    )
    dscores = probs * (dprobs - over_keys(probs * dprobs, jnp.add)) * (1.0 / math.sqrt(HEAD_DIM))
    for key in range(TOKENS):
        weight = by_token(one_key(probs, key, spread, nodes))
        dheads_ref[key, :, 2 * columns :] = jnp.sum(weight * dmixed_ref[...], axis=0)
        weight = by_token(one_key(dscores, key, spread, nodes))
        dheads_ref[key, :, columns : 2 * columns] = jnp.sum(
            weight * heads_ref[:, :, :columns], axis=0
        )
        term = weight * heads_ref[key, :, columns : 2 * columns][None]
        dheads_ref[:, :, :columns] = term if key == 0 else dheads_ref[:, :, :columns] + term
    back_h[...], back_l[...] = split(dheads_ref[...])


def input_back_kernel(
    hops_ref,
    z0_ref,
    back_h,
    back_l,
    dz1_ref,
    front_small,
    wi_h,
    wi_l,
    wh_h,
    wh_l,
    gain_attn,
    dhops_ref,
    sums,
):
    nodes = hops_ref.shape[1]
    rows = TOKENS * nodes
    columns = z0_ref.shape[2]
    features = hops_ref.shape[2]
    at_small = features + front_small.shape[0]

    @pl.when(pl.program_id(0) == 0)
    def _():
        sums[...] = jnp.zeros_like(sums)
        sums[features:at_small] = front_small[...]

    def flat(ref):
        return ref[...].reshape(rows, ref.shape[2])

    n1, scale = standard(flat(z0_ref))
    du1 = product((flat(back_h), flat(back_l)), pair(wh_h, wh_l), 1, 1)
    sums[at_small + 1 : at_small + 2] += column_sum(du1 * n1)
    sums[at_small + 2 : at_small + 3] += column_sum(du1)
    dz0 = flat(dz1_ref) + standard_back(du1 * gain_attn[...], n1, scale)
    sums[at_small + 3 : at_small + 4] += column_sum(dz0)
    near = split(dz0)
    sums[:features] += product(split(flat(hops_ref)), near, 0, 0)
    dhops_ref[...] = product(near, pair(wi_h, wi_l), 1, 1).reshape(TOKENS, nodes, features)


def heads_weight_kernel(z0_ref, back_h, back_l, rest, gain_attn, shift_attn, first, second, u_h, u_l):
    nodes = z0_ref.shape[1]
    rows = TOKENS * nodes
    columns = z0_ref.shape[2]

    @pl.when(pl.program_id(0) == 0)
    def _():
        first[...] = jnp.zeros_like(first)
        second[:columns] = jnp.zeros((columns, columns), jnp.float32)
        second[columns:] = rest[...]

    n1, _ = standard(z0_ref[...].reshape(rows, columns))
    u_h[...], u_l[...] = split(n1 * gain_attn[...] + shift_attn[...])
    for third in range(3):
        cut = slice(third * columns, (third + 1) * columns)
        grown = product(
            pair(u_h, u_l),
            (back_h[:, :, cut].reshape(rows, columns), back_l[:, :, cut].reshape(rows, columns)),
            0,
            0,
        )
        if third < 2:
            first[cut] += grown
        else:
            second[:columns] += grown


def split_kernel(*refs):
    count = len(refs) // 3
    for place in range(count):
        source, upper, lower = refs[place], refs[count + 2 * place], refs[count + 2 * place + 1]
        step = min(64, source.shape[0])

        def some(index, _, source=source, upper=upper, lower=lower, step=step):
            rows = pl.ds(pl.multiple_of(index * step, step), step)
            upper[rows, :], lower[rows, :] = split(source[rows, :])
            return 0

        lax.fori_loop(0, source.shape[0] // step, some, 0)


def layer_parts(hops, cotangent, w_input, bias_input, gain_attn, shift_attn, w_heads, w_merge, bias_merge, gain_ffn, shift_ffn, w_expand, bias_expand, w_reduce, bias_reduce, readout):
    tokens, node_count, features = hops.shape
    columns = w_input.shape[1]
    wide = w_expand.shape[1]
    nodes = min(NODES_STEP, node_count)
    rows = tokens * nodes
    f32, bf16 = jnp.float32, jnp.bfloat16

    def shape(*dims, dtype=f32):
        return jax.ShapeDtypeStruct(dims, dtype)

    weights = [w_input, w_heads, w_merge, w_expand, w_reduce]
    halves = pl.pallas_call(
        split_kernel,
        out_shape=[shape(*w.shape, dtype=bf16) for w in weights for _ in range(2)],
        compiler_params=pltpu.CompilerParams(vmem_limit_bytes=40 << 20),
        cost_estimate=work(4),
        name="split_weights",
    )(*weights)
    wi, wh, wm, we, wr = [halves[2 * i : 2 * i + 2] for i in range(5)]

    def fixed(array):
        return pl.BlockSpec(array.shape, lambda step: (0,) * len(array.shape), pipeline_mode=pl.Buffered(1))

    def row(vector):
        return vector.reshape(1, -1)

    def part(*dims):
        return pl.BlockSpec((dims[0], nodes, dims[1]), lambda step: (0, step, 0))

    flat = pl.BlockSpec((nodes, columns), lambda step: (step, 0))
    vectors = [row(v) for v in (bias_input, gain_attn, shift_attn, bias_merge, gain_ffn, shift_ffn, bias_expand, bias_reduce, readout)]
    outs = [
        shape(node_count, columns),
        shape(tokens, node_count, columns),
        shape(tokens, node_count, 3 * columns),
        shape(tokens // 2, node_count, LANES),
        shape(tokens, node_count, columns),
        shape(tokens, node_count, columns),
        shape(wide + columns // 2, columns),
        shape(2 * columns + columns // 2, columns),
        shape(8, columns),
    ]
    out, z0, heads, probs, _, dz1, first, second, front_small = pl.pallas_call(
        front_kernel,
        grid=(node_count // nodes,),
        out_shape=outs,
        in_specs=[part(tokens, features), flat]
        + [fixed(w) for w in (*wi, *wh, *wm, *we, *wr)]
        + [fixed(v) for v in vectors],
        out_specs=[
            flat,
            part(tokens, columns),
            part(tokens, 3 * columns),
            part(tokens // 2, LANES),
            part(tokens, columns),
            part(tokens, columns),
            fixed(outs[6]),
            fixed(outs[7]),
            fixed(outs[8]),
        ],
        scratch_shapes=[
            pltpu.VMEM((rows, columns), bf16),
            pltpu.VMEM((rows, columns), bf16),
            pltpu.VMEM((rows, wide), bf16),
            pltpu.VMEM((rows, wide), bf16),
            pltpu.VMEM((rows, wide), bf16),
            pltpu.VMEM((rows, wide), bf16),
            pltpu.VMEM((rows, wide), f32),
            pltpu.VMEM((rows, columns), f32),
            pltpu.VMEM((rows, columns), f32),
        ],
        compiler_params=pltpu.CompilerParams(vmem_limit_bytes=56 << 20),
        cost_estimate=work(52),
        name="layer_front",
    )(hops, cotangent, *wi, *wh, *wm, *we, *wr, *vectors)
    steps = node_count // nodes

    def attention_back(dz1, start, count, so_far):
        def some(*dims):
            return pl.BlockSpec((dims[0], nodes, dims[1]), lambda step: (0, step + start, 0))

        given = [heads, probs, dz1, *wm, *so_far]
        return pl.pallas_call(
            attention_back_kernel,
            grid=(count,),
            out_shape=[shape(tokens, node_count, 3 * columns, dtype=bf16)] * 2,
            in_specs=[
                some(tokens, 3 * columns),
                some(tokens // 2, LANES),
                some(tokens, columns),
                *[fixed(w) for w in wm],
                *[pl.BlockSpec(memory_space=pl.ANY) for _ in so_far],
            ],
            out_specs=[some(tokens, 3 * columns)] * 2,
            scratch_shapes=[
                pltpu.VMEM((tokens, nodes, columns), f32),
                pltpu.VMEM((tokens, nodes, 3 * columns), f32),
            ],
            input_output_aliases={5: 0, 6: 1} if so_far else {},
            compiler_params=pltpu.CompilerParams(vmem_limit_bytes=40 << 20),
            cost_estimate=work(5 * count),
            name="attention_back",
        )(*given)

    def input_back(back):
        given = [hops, z0, *back, dz1, front_small, *wi, *wh, vectors[1]]
        sums = shape(-(-(features + 16) // SHARE) * SHARE, columns)
        return pl.pallas_call(
            input_back_kernel,
            grid=(steps,),
            out_shape=[shape(tokens, node_count, features), sums],
            in_specs=[
                part(tokens, features),
                part(tokens, columns),
                part(tokens, 3 * columns),
                part(tokens, 3 * columns),
                part(tokens, columns),
                *[fixed(g) for g in given[5:]],
            ],
            out_specs=[part(tokens, features), fixed(sums)],
            compiler_params=pltpu.CompilerParams(vmem_limit_bytes=40 << 20),
            cost_estimate=work(10),
            name="input_back",
        )(*given)

    def heads_weight(back, rest):
        given = [z0, *back, rest, *vectors[1:3]]
        outs = [shape(2 * columns, columns), shape(columns + rest.shape[0], columns)]
        return pl.pallas_call(
            heads_weight_kernel,
            grid=(steps,),
            out_shape=outs,
            in_specs=[
                part(tokens, columns),
                part(tokens, 3 * columns),
                part(tokens, 3 * columns),
                *[fixed(g) for g in given[3:]],
            ],
            out_specs=[fixed(o) for o in outs],
            scratch_shapes=[pltpu.VMEM((rows, columns), bf16)] * 2,
            compiler_params=pltpu.CompilerParams(vmem_limit_bytes=40 << 20),
            cost_estimate=work(8),
            name="heads_weight",
        )(*given)

    return out, dz1, [first, second], steps, attention_back, input_back, heads_weight


CORE, Y, NEAR_Z, FAR_Z, X = ("row", 1), ("row", 2), ("row", 4), ("row", 8), ("col", 1)
ORDERS = ((CORE, X, Y, NEAR_Z, FAR_Z), (CORE, Y, X, NEAR_Z, FAR_Z))
SHARE = 256


def swap(values, stage):
    axis, distance = stage
    size = lax.axis_size(axis)
    return lax.ppermute(values, axis, [(place, place ^ distance) for place in range(size)])


def side(stage):
    axis, distance = stage
    return lax.axis_index(axis) // distance % 2


def tie(*values):
    return lax.optimization_barrier(values)


def halves(parts, step):
    kept, sent = [], []
    for part, order in zip(parts, ORDERS):
        half = part.shape[0] // 2
        mine = side(order[step])
        kept.append(lax.dynamic_slice_in_dim(part, mine * half, half))
        sent.append(lax.dynamic_slice_in_dim(part, (1 - mine) * half, half))
    return kept, sent


def swap_all(parts, step):
    return [swap(part, order[step]) for part, order in zip(parts, ORDERS)]


def add_all(left, right):
    return [a + b for a, b in zip(left, right)]


def reduce_step(parts, step):
    kept, sent = halves(parts, step)
    return add_all(kept, swap_all(sent, step))


def join_step(parts, step):
    return [jnp.concatenate([a, b], axis=0) for a, b in zip(parts, swap_all(parts, step))]


def last_join(parts):
    return [piece for both in zip(parts, swap_all(parts, 0)) for piece in both]


def part_places():
    found = []
    for order in ORDERS:
        place = jnp.int32(0)
        for stage in order:
            place = 2 * place + side(stage)
        found.append(place)
    return jnp.stack(found)


def gather_pieces(places_ref, pieces, whole):
    start = 0
    for part in range(2):
        count = 16
        size = pieces[2 * part].shape[0] // count
        for turn in range(2):
            for piece in range(count):
                target = ((turn * count + piece) ^ places_ref[part]) * size + start
                whole[pl.ds(pl.multiple_of(target, 8), size), :] = pieces[2 * part + turn][
                    piece * size : (piece + 1) * size
                ]
        start += 2 * count * size


def front_outputs(places_ref, *refs):
    pieces, (grad_reduce, grad_expand, grad_merge, whole) = refs[:4], refs[4:]
    gather_pieces(places_ref, pieces, whole)
    split_front(whole, grad_reduce, grad_expand, grad_merge)


def split_front(whole, grad_reduce, grad_expand, grad_merge):
    wide, columns = grad_reduce.shape
    part = columns // 2
    grad_reduce[...] = whole[:wide]
    grad_merge[:part] = whole[wide : wide + part]
    start = wide + part
    grad_expand[:, :columns] = whole[start : start + columns]
    grad_expand[:, columns:] = whole[start + columns : start + 2 * columns]
    grad_merge[part:] = whole[start + 2 * columns :]


def back_outputs(places_ref, *refs):
    pieces, whole = refs[:4], refs[-1]
    gather_pieces(places_ref, pieces, whole)
    split_back(whole, *refs[4:-1])


def split_back(whole, grad_heads, grad_input, *vectors):
    columns = grad_heads.shape[0]
    for third in range(3):
        grad_heads[:, third * columns : (third + 1) * columns] = whole[
            third * columns : (third + 1) * columns
        ]
    start = 3 * columns
    grad_input[...] = whole[start : start + grad_input.shape[0]]
    start += grad_input.shape[0]
    for vector, row in zip(vectors, SMALL_ROWS):
        vector[:, :columns] = whole[start + row : start + row + 1]
    vectors[2][:, columns:] = whole[start + 5 : start + 6]


SMALL_ROWS = (0, 1, 2, 3, 4, 6, 9, 10, 11)


def outputs(kernel, name, places, pieces, shapes, rows, columns):
    return pl.pallas_call(
        kernel,
        out_shape=[jax.ShapeDtypeStruct(s, jnp.float32) for s in shapes],
        in_specs=[pl.BlockSpec(memory_space=pltpu.SMEM)]
        + [pl.BlockSpec(memory_space=pltpu.VMEM)] * len(pieces),
        out_specs=[pl.BlockSpec(memory_space=pltpu.VMEM)] * len(shapes),
        scratch_shapes=[pltpu.VMEM((rows, columns), jnp.float32)],
        compiler_params=pltpu.CompilerParams(vmem_limit_bytes=48 << 20),
        cost_estimate=work(4),
        name=name,
    )(places, *pieces)


def join_two(first, second, whole):
    whole[: first.shape[0]] = first[...]
    whole[first.shape[0] :] = second[...]


def front_whole(places_ref, first, second, *refs):
    join_two(first, second, refs[-1])
    split_front(refs[-1], *refs[:-1])


def back_whole(places_ref, first, second, *refs):
    join_two(first, second, refs[-1])
    split_back(refs[-1], *refs[:-1])


def per_device(
    node_features,
    block_values,
    block_rows,
    block_cols,
    block_count,
    w_input,
    bias_input,
    gain_attn,
    shift_attn,
    w_heads,
    w_merge,
    bias_merge,
    gain_ffn,
    shift_ffn,
    w_expand,
    bias_expand,
    w_reduce,
    bias_reduce,
    readout,
    cotangent,
):
    values = block_values[0, 0]
    row_ids = block_rows[0, 0]
    col_ids = block_cols[0, 0]
    block_size = values.shape[-1]
    node_count = node_features.shape[0]
    row_blocks = lax.axis_size("col") * node_count // block_size
    col_blocks = lax.axis_size("row") * node_count // block_size
    is_live = (jnp.arange(values.shape[0]) < block_count[0, 0]).astype(jnp.float32)
    row_table = (row_ids[:, None] == jnp.arange(row_blocks)[None, :]).astype(jnp.float32) * is_live[
        :, None
    ]
    col_table = (col_ids[:, None] == jnp.arange(col_blocks)[None, :]).astype(jnp.float32) * is_live[
        :, None
    ]
    devices = lax.axis_size("row") * lax.axis_size("col")
    whole = (
        block_size == LANES
        and node_count == LANES
        and node_features.shape[1] == PIECE * devices
        and devices * values.size * 4 <= 16 << 20
    )
    if whole:
        n_col = lax.axis_size("col")
        everything = lax.all_gather(values, AXES, axis=0, tiled=True)
        places = jnp.concatenate([row_ids, col_ids, block_count[0]]).astype(jnp.float32)
        note = jnp.zeros((PIECE, LANES), jnp.float32).at[0, : places.shape[0]].set(places)
        sent = jnp.concatenate(
            [
                node_features.T.reshape(devices, PIECE, LANES),
                jnp.broadcast_to(note[None], (devices, PIECE, LANES)),
            ],
            axis=1,
        )
        taken = lax.all_to_all(sent, AXES, 0, 0, tiled=True)
        meta = taken[:, PIECE, : places.shape[0]].astype(jnp.int32)
        walked = walk(True, meta, taken, everything, n_col, row_blocks)
        walked = lax.all_to_all(walked, AXES, 0, 0, tiled=True)
        stacked = walked.reshape(devices, TOKENS, PIECE, LANES).transpose(1, 3, 0, 2)
        stacked = stacked.reshape(TOKENS, LANES, devices * PIECE)
    else:
        hop_list = [node_features]
        for hop_index in range(HOPS):
            field = hop_list[-1]
            forward_columns = field.shape[1]
            forward_gathered = lax.all_gather(field, "row", axis=0, tiled=True).reshape(
                col_blocks, block_size, forward_columns
            )
            forward_picked = forward_gathered[col_ids]
            forward_products = jnp.einsum("bij,bjw->biw", values, forward_picked, precision=exact)
            forward_partial_value = jnp.einsum(
                "br,biw->riw", row_table, forward_products, precision=exact
            ).reshape(row_blocks * block_size, forward_columns)
            hop_list.append(
                lax.psum_scatter(forward_partial_value, "col", scatter_dimension=0, tiled=True)
            )
        stacked = jnp.stack(hop_list, axis=0)

    layer_out, dz1, front, steps, attention_back, input_back, heads_weight = layer_parts(
        stacked,
        cotangent,
        w_input,
        bias_input,
        gain_attn,
        shift_attn,
        w_heads,
        w_merge,
        bias_merge,
        gain_ffn,
        shift_ffn,
        w_expand,
        bias_expand,
        w_reduce,
        bias_reduce,
        readout,
    )
    columns, wide = w_expand.shape
    if whole and lax.axis_size("row") == 16 and n_col == 2:
        kept, sent = halves(front, 0)
        sent, dz1 = tie(sent, dz1)
        taken = swap_all(sent, 0)
        early = attention_back(dz1, 0, steps // 2, ())
        kept, taken, early = tie(kept, taken, early)
        kept, sent = halves(add_all(kept, taken), 1)
        sent, dz1, early = tie(sent, dz1, early)
        taken = swap_all(sent, 1)
        back = attention_back(dz1, steps // 2, steps - steps // 2, early)
        grad_hops, rest = input_back(back)
        kept, taken, grad_hops, rest = tie(kept, taken, grad_hops, rest)
        kept, sent = halves(add_all(kept, taken), 2)
        away = grad_hops.reshape(TOKENS, LANES, devices, PIECE).transpose(2, 0, 3, 1)
        away = away.reshape(devices, TOKENS * PIECE, LANES)
        sent, away, back = tie(sent, away, back)
        taken = swap_all(sent, 2)
        away = lax.all_to_all(away, AXES, 0, 0, tiled=True)
        late = heads_weight(back, rest)
        kept, taken, late = tie(kept, taken, late)
        front = add_all(kept, taken)
        front = reduce_step(front, 3)
        late = reduce_step(late, 0)
        kept, sent = halves(front, 4)
        late_kept, late_sent = halves(late, 1)
        sent, late_sent, away = tie(sent, late_sent, away)
        taken, late_taken = swap_all(sent, 4), swap_all(late_sent, 1)
        home = walk(False, meta, away, everything, n_col, row_blocks)
        taken, late_taken, home = tie(taken, late_taken, home)
        home = lax.all_to_all(home, AXES, 0, 0, tiled=True)[:, :PIECE]
        carried = grad_hops[0] + home.reshape(devices * PIECE, LANES).T
        front = add_all(kept, taken)
        late = add_all(late_kept, late_taken)
        for step in (2, 3, 4):
            late = reduce_step(late, step)
        for step in (4, 3, 2, 1):
            front = join_step(front, step)
            late = join_step(late, step)
        front, late, order = last_join(front), last_join(late), part_places()
        kernels = front_outputs, back_outputs
    else:
        back = attention_back(dz1, 0, steps, ())
        grad_hops, rest = input_back(back)
        late = heads_weight(back, rest)
        carried = grad_hops[HOPS]
        for hop_index in range(HOPS - 1, -1, -1):
            gathered = lax.all_gather(carried, "col", axis=0, tiled=True).reshape(
                row_blocks, block_size, carried.shape[1]
            )
            picked = gathered[row_ids]
            products = jnp.einsum("bji,bjw->biw", values, picked, precision=exact)
            partial_value = jnp.einsum("bc,biw->ciw", col_table, products, precision=exact)
            carried = grad_hops[hop_index] + lax.psum_scatter(
                partial_value.reshape(col_blocks * block_size, carried.shape[1]),
                "row",
                scatter_dimension=0,
                tiled=True,
            )
        front, late = lax.psum((front, late), AXES)
        order = jnp.zeros((2,), jnp.int32)
        kernels = front_whole, back_whole
    front_shapes = [(wide, columns), (columns, wide), (columns, columns)]
    back_shapes = [(columns, 3 * columns), w_input.shape]
    back_shapes += [(1, wide if row == 2 else columns) for row in SMALL_ROWS]
    front_rows = wide + 3 * columns
    back_rows = 3 * columns + rest.shape[0]
    grad_w_reduce, grad_w_expand, grad_w_merge = outputs(
        kernels[0], "front_outputs", order, front, front_shapes, front_rows, columns
    )
    grad_w_heads, grad_w_input, *vectors = outputs(
        kernels[1], "back_outputs", order, late, back_shapes, back_rows, columns
    )
    (
        grad_readout,
        grad_bias_reduce,
        grad_bias_expand,
        grad_gain_ffn,
        grad_shift_ffn,
        grad_bias_merge,
        grad_gain_attn,
        grad_shift_attn,
        grad_bias_input,
    ) = [vector.reshape(-1) for vector in vectors]
    return (
        layer_out,
        carried,
        grad_w_input,
        grad_bias_input,
        grad_gain_attn,
        grad_shift_attn,
        grad_w_heads,
        grad_w_merge,
        grad_bias_merge,
        grad_gain_ffn,
        grad_shift_ffn,
        grad_w_expand,
        grad_bias_expand,
        grad_w_reduce,
        grad_bias_reduce,
        grad_readout,
    )


def solution(mesh):
    placed = (
        P(("row", "col"), None),
        P("row", "col", None, None, None),
        P("row", "col", None),
        P("row", "col", None),
        P("row", "col"),
        P(),
        P(),
        P(),
        P(),
        P(),
        P(),
        P(),
        P(),
        P(),
        P(),
        P(),
        P(),
        P(),
        P(),
        P(("row", "col"), None),
    )
    return jax.shard_map(
        per_device,
        mesh=mesh,
        in_specs=placed,
        out_specs=(
            P(("row", "col"), None),
            P(("row", "col"), None),
            P(),
            P(),
            P(),
            P(),
            P(),
            P(),
            P(),
            P(),
            P(),
            P(),
            P(),
            P(),
            P(),
            P(),
        ),
        check_vma=False,
    )
```
